32 devices in a mesh: seg: 2 (over y), ch: 16 (over z, x, core).
Axes of the slice: x: 2, y: 2, z: 4, core: 2. Of those that a mesh axis runs over, the one named last changes fastest.
Arguments:
- strain: float32 [2, 1024, 2048], P('seg', 'ch')
- ref_local: int32 [4, 16], replicated, may hold values from 0 to 127, as said below
- owners: int32 [4], replicated, may hold values from 0 to 15, as said below
Outputs:
- toeplitz_blocks: float32 [64, 2048, 64], P('seg', 'ch')
The draws below stay inside these ranges and needn't reach their ends.
Inputs may be any that keep to these rules, and one draw needn't show every extreme that they name: `ref_local`: each row holds 16 distinct offsets; the first row holds 127. `owners`: the 4 entries are distinct, and one of them is 15.
All inputs are finite; a program needn't handle non-finite values.
Results may differ from the reference program's by a relative error of at most 0.0029.
Values may be sent and summed in bfloat16 or wider, within the bound.
A program may use at most 64 MiB of HBM per device.

```python
import math
import jax
import jax.numpy as jnp
from jax import lax

C = 2048
L = 64
PANELS = 4
PANEL_W = 16
SEGS = 2
S = 1024
C_DEV = 128
R = 64


def draw_strain(key, part):
    keys = jax.random.split(key, 6)
    n_modes = 6
    times = jnp.arange(S, dtype=jnp.float32)[None, :, None]
    freqs = jnp.exp(jax.random.uniform(keys[0], (n_modes,), jnp.float32, math.log(0.003), math.log(0.6)))
    amps = jax.random.normal(keys[1], (SEGS, 1, C, n_modes), jnp.float32) * 0.12
    phases = jax.random.uniform(keys[2], (SEGS, 1, C, n_modes), jnp.float32, -math.pi, math.pi)
    offsets = jax.random.normal(keys[3], (SEGS, 1, C), jnp.float32) * 3.0
    slopes = jax.random.normal(keys[4], (SEGS, 1, C), jnp.float32) * 3.0
    ramp = 2.0 * times / S - 1.0
    signal_sum = offsets + slopes * ramp
    for mode_id in range(n_modes):
        signal_sum = signal_sum + amps[..., mode_id] * jnp.sin(freqs[mode_id] * times + phases[..., mode_id])
    noise = jax.random.normal(keys[5], (SEGS, S, C), jnp.float32)
    return signal_sum + noise


def draw_ref_local(key, part):
    base_key = jax.random.fold_in(key, 11)
    keys = jax.random.split(base_key, PANELS)
    order_keys = jax.random.split(jax.random.fold_in(base_key, 5), PANELS)
    rows = jax.vmap(lambda one_key: jax.random.permutation(one_key, C_DEV)[:PANEL_W])(keys).astype(jnp.int32)
    first_shift = C_DEV - 1 - rows[0, 0]
    shifts = jnp.zeros((PANELS,), jnp.int32).at[0].set(first_shift)
    rows = (rows + shifts[:, None]) % C_DEV
    return jax.vmap(lambda one_key, one_row: jax.random.permutation(one_key, one_row))(order_keys, rows).astype(jnp.int32)


def draw_owners(key, part):
    base_key = jax.random.fold_in(key, 23)
    picked = jax.random.permutation(base_key, C // C_DEV)[:PANELS].astype(jnp.int32)
    n_groups = C // C_DEV
    picked = (picked + (n_groups - 1) - picked[0]) % n_groups
    return jax.random.permutation(jax.random.fold_in(base_key, 7), picked).astype(jnp.int32)


def setup_inputs(seed: int = 0) -> dict:
    streams_of = jax.random.split(jax.random.key(seed), 4)
    strain = draw_strain(jax.random.fold_in(streams_of[3], 71), 0)
    ref_local = draw_ref_local(jax.random.fold_in(streams_of[3], 71), 0)
    owners = draw_owners(jax.random.fold_in(streams_of[3], 71), 0)
    return dict(strain=strain, ref_local=ref_local, owners=owners)


def detrend_cols(series):
    n_total = series.shape[0]
    mid_time = (n_total - 1) / 2.0
    spread = n_total * (n_total * n_total - 1) / 12.0
    centred = (jnp.arange(n_total, dtype=jnp.float32) - mid_time)[:, None]
    level_val = jnp.sum(series, axis=0) / n_total
    slope_val = jnp.sum(centred * series, axis=0) / spread
    return (series - level_val - slope_val * centred).astype(jnp.bfloat16)


def reference(strain, ref_local, owners):
    ref_cols = (owners[:, None] * C_DEV + ref_local).reshape(-1).astype(jnp.int32)

    def one_segment(running, series):
        cleaned = detrend_cols(series).astype(jnp.float32)
        ref_data = jnp.take(cleaned, ref_cols, axis=1)
        padded = jnp.concatenate([cleaned, jnp.zeros((L, C), jnp.float32)], axis=0)

        def one_lag(lag_pos):
            shifted = lax.dynamic_slice_in_dim(padded, lag_pos, S, 0)
            return lax.dot_general(shifted, ref_data, (((0,), (0,)), ((), ())), precision=lax.Precision.HIGHEST)

        lag_covs = lax.map(one_lag, jnp.arange(L, dtype=jnp.int32))
        return running + lag_covs, None

    summed, _ = lax.scan(one_segment, jnp.zeros((L, C, R), jnp.float32), strain)
    lag_ids = jnp.arange(L, dtype=jnp.float32)
    return summed / (SEGS * (S - lag_ids))[:, None, None]
```

```python
import functools
import math

import jax
import jax.numpy as jnp
from jax import lax
from jax.experimental import pallas as pl
from jax.experimental.pallas import tpu as pltpu
from jax.sharding import PartitionSpec as P

L = 64
LANES = 128
SHIFTS = 16
MESH = pl.DeviceIdType.MESH


def spread_2(block, axis, holder):
    block = jnp.where(lax.axis_index(axis) == holder, block, jnp.zeros_like(block))
    return lax.psum(block, axis)


def detrend_cols(series):
    n_total = series.shape[0]
    mid_time = (n_total - 1) / 2.0
    spread = n_total * (n_total * n_total - 1) / 12.0
    centred = (jnp.arange(n_total, dtype=jnp.float32) - mid_time)[:, None]
    level_val = jnp.sum(series, axis=0) / n_total
    slope_val = jnp.sum(centred * series, axis=0) / spread
    return (series - level_val - slope_val * centred).astype(jnp.bfloat16)


def owner_panels(detrended, ref_local, owners):
    pieces = []
    for panel_id in range(ref_local.shape[0]):
        own_cols = jnp.take(detrended, ref_local[panel_id], axis=1)
        pieces.append(spread_2(own_cols, "ch", owners[panel_id]))
    return jnp.concatenate(pieces, axis=1)


def narrow_blocks(strain, ref_local, owners):
    my_rows = strain[0]
    s_dev, chans = my_rows.shape
    n_ch = lax.axis_size("ch")
    n_seg = lax.axis_size("seg")
    n_total = s_dev * n_ch
    c_dev = chans // n_ch
    series = lax.all_to_all(my_rows, "ch", split_axis=1, concat_axis=0, tiled=True)
    detrended = detrend_cols(series)
    panels = owner_panels(detrended, ref_local, owners)
    width_ref = panels.shape[1]
    padded = jnp.concatenate([detrended, jnp.zeros((L, c_dev), jnp.bfloat16)], axis=0)
    blk_rows = min(512, n_total)
    n_blocks = n_total // blk_rows
    lag_dev = L // n_seg
    lag_count = lax.axis_size("seg") * lag_dev

    def add_block(blk_idx, running):
        blk_start = blk_idx * blk_rows
        window = lax.dynamic_slice_in_dim(padded, blk_start, blk_rows + lag_count - 1, 0)
        lagged = jnp.concatenate(
            [window[lag_off : lag_off + blk_rows] for lag_off in range(lag_count)], axis=1
        )
        ref_block = lax.dynamic_slice_in_dim(panels, blk_start, blk_rows, 0)
        return running + lax.dot_general(
            lagged, ref_block, (((0,), (0,)), ((), ())), preferred_element_type=jnp.float32
        )

    start_acc = jnp.zeros((lag_count * c_dev, width_ref), jnp.float32)
    running = lax.fori_loop(0, n_blocks, add_block, start_acc)
    summed = lax.psum_scatter(
        running.reshape(lag_count, c_dev, width_ref), "seg", scatter_dimension=0, tiled=True
    )
    lag_ids = (lax.axis_index("seg") * lag_dev + jnp.arange(lag_dev, dtype=jnp.int32)).astype(
        jnp.float32
    )
    return summed / (n_seg * (n_total - lag_ids))[:, None, None]


def exchange_kernel(
    n_seg, n_ch, group,
    strain_hbm, owners_ref, local_ref, d_out, r_out,
    mine, raw, rline, d_all, r_all,
    load_sem, own_sem, a_send, a_recv, z_send, z_recv, p_send, p_recv, d_send, d_recv, r_send, r_recv,
):
    seg = lax.axis_index("seg")
    me = lax.axis_index("ch")
    high, low = me // group, me % group
    n_high = n_ch // group
    s_dev = strain_hbm.shape[0]
    c_dev = strain_hbm.shape[1] // n_ch
    half = s_dev // 2
    n_total = s_dev * n_ch
    n_panels, panel_w = local_ref.shape
    width = n_panels * panel_w

    barrier = pltpu.get_barrier_semaphore()
    for k in range(1, n_ch):
        pl.semaphore_signal(
            barrier, inc=1, device_id=(seg, (me + k) % n_ch), device_id_type=MESH
        )
    for k in range(1, n_seg):
        pl.semaphore_signal(
            barrier, inc=1, device_id=((seg + k) % n_seg, me), device_id_type=MESH
        )

    load = pltpu.make_async_copy(strain_hbm, mine, load_sem)
    load.start()
    cols = pl.ds(pl.multiple_of(me * c_dev, LANES), c_dev)
    own = pltpu.make_async_copy(strain_hbm.at[:, cols], raw.at[me], own_sem)
    own.start()
    load.wait()

    blocks = []
    for p in range(n_panels):
        holder = jnp.full((s_dev, c_dev), owners_ref[p], jnp.int32)
        block = jnp.zeros((s_dev, c_dev), jnp.float32)
        for o in range(n_ch):
            block = jnp.where(holder == o, mine[:, o * c_dev : (o + 1) * c_dev], block)
        blocks.append(block)
    blocks = jnp.concatenate(blocks, axis=1)
    targets = jnp.concatenate(
        [local_ref[p : p + 1, :] + p * c_dev for p in range(n_panels)], axis=1
    )
    hot = (
        lax.broadcasted_iota(jnp.int32, (n_panels * c_dev, width), 0) == targets
    ).astype(jnp.float32)
    picked = jnp.dot(
        blocks, hot, precision=lax.Precision.HIGHEST, preferred_element_type=jnp.float32
    )
    rline[low, high] = jnp.concatenate([picked[:half], picked[half:]], axis=1)

    pl.semaphore_wait(barrier, n_ch - 1 + n_seg - 1)

    z_copies = []
    for k in range(1, n_high):
        z_copies.append(
            pltpu.make_async_remote_copy(
                src_ref=rline.at[low, high],
                dst_ref=rline.at[low, high],
                send_sem=z_send.at[k],
                recv_sem=z_recv.at[k],
                device_id=(seg, ((high + k) % n_high) * group + low),
                device_id_type=MESH,
            )
        )
        z_copies[-1].start()
    a_copies = []
    for k in range(1, n_ch):
        dst = (me + k) % n_ch
        a_copies.append(
            pltpu.make_async_remote_copy(
                src_ref=strain_hbm.at[:, pl.ds(pl.multiple_of(dst * c_dev, LANES), c_dev)],
                dst_ref=raw.at[me],
                send_sem=a_send.at[k],
                recv_sem=a_recv.at[k],
                device_id=(seg, dst),
                device_id_type=MESH,
            )
        )
        a_copies[-1].start()

    for copy in z_copies:
        copy.wait()
    p_copies = []
    for k in range(1, group):
        p_copies.append(
            pltpu.make_async_remote_copy(
                src_ref=rline.at[low],
                dst_ref=rline.at[low],
                send_sem=p_send.at[k],
                recv_sem=p_recv.at[k],
                device_id=(seg, high * group + (low + k) % group),
                device_id_type=MESH,
            )
        )
        p_copies[-1].start()
    mid_time = (n_total - 1) / 2.0
    spread = n_total * (n_total * n_total - 1) / 12.0

    for copy in p_copies:
        copy.wait()
    rows = jnp.concatenate(
        [rline[i % group, i // group] for i in range(n_ch)], axis=0
    )
    row_id = lax.broadcasted_iota(jnp.int32, (n_ch * half, LANES), 0)
    upper = (lax.broadcasted_iota(jnp.int32, (n_ch * half, LANES), 1) >= width).astype(jnp.int32)
    times = (row_id // half) * s_dev + row_id % half + upper * half
    centred = times.astype(jnp.float32) - mid_time
    level = jnp.sum(rows, axis=0, keepdims=True)
    slope = jnp.sum(centred * rows, axis=0, keepdims=True)
    level = (level + jnp.concatenate([level[:, width:], level[:, :width]], axis=1)) / n_total
    slope = (slope + jnp.concatenate([slope[:, width:], slope[:, :width]], axis=1)) / spread
    r_all[seg] = (rows - level - slope * centred).astype(jnp.bfloat16)
    r_copies = []
    for k in range(1, n_seg):
        r_copies.append(
            pltpu.make_async_remote_copy(
                src_ref=r_all.at[seg],
                dst_ref=r_all.at[seg],
                send_sem=r_send.at[k],
                recv_sem=r_recv.at[k],
                device_id=((seg + k) % n_seg, me),
                device_id_type=MESH,
            )
        )
        r_copies[-1].start()

    own.wait()
    for copy in a_copies:
        copy.wait()
    series = raw[...].reshape(n_total, c_dev)
    centred = lax.broadcasted_iota(jnp.int32, (n_total, c_dev), 0).astype(jnp.float32) - mid_time
    level = jnp.sum(series, axis=0, keepdims=True) / n_total
    slope = jnp.sum(centred * series, axis=0, keepdims=True) / spread
    d_all[seg] = (series - level - slope * centred).astype(jnp.bfloat16)
    d_copies = []
    for k in range(1, n_seg):
        d_copies.append(
            pltpu.make_async_remote_copy(
                src_ref=d_all.at[seg],
                dst_ref=d_all.at[seg],
                send_sem=d_send.at[k],
                recv_sem=d_recv.at[k],
                device_id=((seg + k) % n_seg, me),
                device_id_type=MESH,
            )
        )
        d_copies[-1].start()
    for copy in r_copies:
        copy.wait()
    r_out[...] = r_all[...]
    for copy in d_copies:
        copy.wait()
    d_out[...] = d_all[...]


def lag_kernel(n_seg, half, d_ref, r_ref, out_ref, d_pad, shifted):
    lag_dev, width, c_dev = out_ref.shape
    n_total = d_ref.shape[1]
    n_ch = n_total // (2 * half)
    seg = lax.axis_index("seg")
    steps = lag_dev // SHIFTS
    d_pad[:, n_total:, :] = jnp.zeros((n_seg, L, c_dev), d_pad.dtype)
    d_pad[:, :n_total, :] = d_ref[...]
    shifted[:, : SHIFTS + 8, :] = jnp.zeros((n_seg, SHIFTS + 8, LANES), jnp.float32)
    lefts, rights = [], []
    for s in range(n_seg):
        packed = r_ref[s].astype(jnp.float32)
        swapped = pltpu.roll(packed, width, 1)
        both = jnp.concatenate(
            [packed.reshape(n_ch, half, LANES), swapped.reshape(n_ch, half, LANES)], axis=1
        ).reshape(n_total, LANES)
        turned = jnp.concatenate(
            [swapped.reshape(n_ch, half, LANES), packed.reshape(n_ch, half, LANES)], axis=1
        ).reshape(n_total, LANES)
        shifted[s, pl.ds(SHIFTS, n_total), 0:width] = both[:, :width]
        shifted[s, pl.ds(SHIFTS + 1, n_total), width:LANES] = turned[:, width:]
        lefts.append(
            jnp.concatenate(
                [
                    d_pad[
                        s,
                        pl.ds(pl.multiple_of(seg * lag_dev + a * SHIFTS, SHIFTS), n_total),
                        :,
                    ]
                    for a in range(steps)
                ],
                axis=1,
            )
        )
    base = (seg * lag_dev).astype(jnp.float32)
    quad = 4
    for j in range(SHIFTS // quad):
        total = None
        for s in range(n_seg):
            right = jnp.concatenate(
                [
                    shifted[s, pl.ds(SHIFTS - quad * j - b, n_total), :].astype(jnp.bfloat16)
                    for b in range(0, quad, 2)
                ],
                axis=1,
            )
            part = lax.dot_general(
                lefts[s], right, (((0,), (0,)), ((), ())), preferred_element_type=jnp.float32
            )
            total = part if total is None else total + part
        turned = total.T
        for a in range(steps):
            for b in range(quad):
                k = a * SHIFTS + j * quad + b
                block = turned[b * width : (b + 1) * width, a * c_dev : (a + 1) * c_dev]
                out_ref[k] = block / (n_seg * (n_total - (base + k)))


def wide_blocks(strain, ref_local, owners):
    my_rows = strain[0]
    s_dev, chans = my_rows.shape
    n_ch = lax.axis_size("ch")
    n_seg = lax.axis_size("seg")
    n_total = s_dev * n_ch
    c_dev = chans // n_ch
    half = s_dev // 2
    group = max(g for g in range(1, math.isqrt(n_ch) + 1) if n_ch % g == 0)
    n_high = n_ch // group
    width = ref_local.shape[0] * ref_local.shape[1]
    vmem = pl.BlockSpec(memory_space=pltpu.VMEM)
    dma = pltpu.SemaphoreType.DMA
    d_shape = (n_seg, n_total, c_dev)
    r_shape = (n_seg, n_ch * half, LANES)
    d_all, r_all = pl.pallas_call(
        functools.partial(exchange_kernel, n_seg, n_ch, group),
        out_shape=(
            jax.ShapeDtypeStruct(d_shape, jnp.bfloat16),
            jax.ShapeDtypeStruct(r_shape, jnp.bfloat16),
        ),
        in_specs=[
            pl.BlockSpec(memory_space=pl.ANY),
            pl.BlockSpec(memory_space=pltpu.SMEM),
            vmem,
        ],
        out_specs=(vmem, vmem),
        scratch_shapes=[
            pltpu.VMEM((s_dev, chans), jnp.float32),
            pltpu.VMEM((n_ch, s_dev, c_dev), jnp.float32),
            pltpu.VMEM((group, n_high, half, LANES), jnp.float32),
            pltpu.VMEM(d_shape, jnp.bfloat16),
            pltpu.VMEM(r_shape, jnp.bfloat16),
            dma, dma,
            dma((n_ch,)), dma((n_ch,)),
            dma((n_high,)), dma((n_high,)),
            dma((group,)), dma((group,)),
            dma((n_seg,)), dma((n_seg,)),
            dma((n_seg,)), dma((n_seg,)),
        ],
        compiler_params=pltpu.CompilerParams(collective_id=0, has_side_effects=True),
    )(my_rows, owners, ref_local)
    turned = pl.pallas_call(
        functools.partial(lag_kernel, n_seg, half),
        out_shape=jax.ShapeDtypeStruct((L // n_seg, width, c_dev), jnp.float32),
        in_specs=[vmem, vmem],
        out_specs=vmem,
        scratch_shapes=[
            pltpu.VMEM((n_seg, n_total + L, c_dev), jnp.bfloat16),
            pltpu.VMEM((n_seg, SHIFTS + n_total + 8, LANES), jnp.float32),
        ],
    )(d_all, r_all)
    return turned.transpose(0, 2, 1)


def solution(mesh):
    n_seg, n_ch = mesh.shape["seg"], mesh.shape["ch"]

    def per_device(strain, ref_local, owners):
        s_dev, chans = strain.shape[1:]
        fits = (
            (chans // n_ch) % LANES == 0
            and (L // n_seg) % SHIFTS == 0
            and s_dev % 32 == 0
            and 2 * ref_local.size == LANES
        )
        return (wide_blocks if fits else narrow_blocks)(strain, ref_local, owners)

    in_specs = (P("seg", "ch", None), P(), P())
    out_specs = P("seg", "ch", None)
    return jax.shard_map(
        per_device, mesh=mesh, in_specs=in_specs, out_specs=out_specs, check_vma=False
    )
```

```python
import functools
import math

import jax
import jax.numpy as jnp
from jax import lax
from jax.experimental import pallas as pl
from jax.experimental.pallas import tpu as pltpu
from jax.sharding import PartitionSpec as P

L = 64
LANES = 128
SHIFTS = 16
GRANT = 24 * 1024 * 1024
MESH = pl.DeviceIdType.MESH


def spread_2(block, axis, holder):
    block = jnp.where(lax.axis_index(axis) == holder, block, jnp.zeros_like(block))
    return lax.psum(block, axis)


def detrend_cols(series):
    n_total = series.shape[0]
    mid_time = (n_total - 1) / 2.0
    spread = n_total * (n_total * n_total - 1) / 12.0
    centred = (jnp.arange(n_total, dtype=jnp.float32) - mid_time)[:, None]
    level_val = jnp.sum(series, axis=0) / n_total
    slope_val = jnp.sum(centred * series, axis=0) / spread
    return (series - level_val - slope_val * centred).astype(jnp.bfloat16)


def owner_panels(detrended, ref_local, owners):
    pieces = []
    for panel_id in range(ref_local.shape[0]):
        own_cols = jnp.take(detrended, ref_local[panel_id], axis=1)
        pieces.append(spread_2(own_cols, "ch", owners[panel_id]))
    return jnp.concatenate(pieces, axis=1)


def narrow_blocks(strain, ref_local, owners):
    my_rows = strain[0]
    s_dev, chans = my_rows.shape
    n_ch = lax.axis_size("ch")
    n_seg = lax.axis_size("seg")
    n_total = s_dev * n_ch
    c_dev = chans // n_ch
    series = lax.all_to_all(my_rows, "ch", split_axis=1, concat_axis=0, tiled=True)
    detrended = detrend_cols(series)
    panels = owner_panels(detrended, ref_local, owners)
    width_ref = panels.shape[1]
    padded = jnp.concatenate([detrended, jnp.zeros((L, c_dev), jnp.bfloat16)], axis=0)
    blk_rows = min(512, n_total)
    n_blocks = n_total // blk_rows
    lag_dev = L // n_seg
    lag_count = lax.axis_size("seg") * lag_dev

    def add_block(blk_idx, running):
        blk_start = blk_idx * blk_rows
        window = lax.dynamic_slice_in_dim(padded, blk_start, blk_rows + lag_count - 1, 0)
        lagged = jnp.concatenate(
            [window[lag_off : lag_off + blk_rows] for lag_off in range(lag_count)], axis=1
        )
        ref_block = lax.dynamic_slice_in_dim(panels, blk_start, blk_rows, 0)
        return running + lax.dot_general(
            lagged, ref_block, (((0,), (0,)), ((), ())), preferred_element_type=jnp.float32
        )

    start_acc = jnp.zeros((lag_count * c_dev, width_ref), jnp.float32)
    running = lax.fori_loop(0, n_blocks, add_block, start_acc)
    summed = lax.psum_scatter(
        running.reshape(lag_count, c_dev, width_ref), "seg", scatter_dimension=0, tiled=True
    )
    lag_ids = (lax.axis_index("seg") * lag_dev + jnp.arange(lag_dev, dtype=jnp.int32)).astype(
        jnp.float32
    )
    return summed / (n_seg * (n_total - lag_ids))[:, None, None]


def exchange_kernel(
    n_seg, n_ch, group,
    strain_hbm, owners_ref, local_ref, d_out, r_out,
    mine, raw, rline, d_all, r_all, stat_out, stat_in,
    load_sem, own_sem, s_send, s_recv, a_send, a_recv, z_send, z_recv, p_send, p_recv,
    d_send, d_recv, r_send, r_recv,
):
    seg = lax.axis_index("seg")
    me = lax.axis_index("ch")
    high, low = me // group, me % group
    n_high = n_ch // group
    s_dev = strain_hbm.shape[0]
    c_dev = strain_hbm.shape[1] // n_ch
    half = s_dev // 2
    n_total = s_dev * n_ch
    n_panels, panel_w = local_ref.shape
    width = n_panels * panel_w
    mid_time = (n_total - 1) / 2.0
    spread = n_total * (n_total * n_total - 1) / 12.0
    order = sorted(range(1, n_ch), key=lambda k: -min(k, n_ch - k))

    def remote(src, dst, sems, k, seg_to, ch_to):
        copy = pltpu.make_async_remote_copy(
            src_ref=src,
            dst_ref=dst,
            send_sem=sems[0].at[k],
            recv_sem=sems[1].at[k],
            device_id=(seg_to, ch_to),
            device_id_type=MESH,
        )
        copy.start()
        return copy

    barrier = pltpu.get_barrier_semaphore()
    for k in order:
        pl.semaphore_signal(
            barrier, inc=1, device_id=(seg, (me + k) % n_ch), device_id_type=MESH
        )
    for k in range(1, n_seg):
        pl.semaphore_signal(
            barrier, inc=1, device_id=((seg + k) % n_seg, me), device_id_type=MESH
        )

    load = pltpu.make_async_copy(strain_hbm, mine, load_sem)
    load.start()
    cols = pl.ds(pl.multiple_of(me * c_dev, LANES), c_dev)
    own = pltpu.make_async_copy(strain_hbm.at[:, cols], raw.at[me], own_sem)
    own.start()
    load.wait()

    my_times = (
        lax.broadcasted_iota(jnp.int32, (s_dev, c_dev), 0) + me * s_dev
    ).astype(jnp.float32) - mid_time
    for o in range(n_ch):
        block = mine[:, o * c_dev : (o + 1) * c_dev]
        stat_out[o] = jnp.concatenate(
            [
                jnp.sum(block, axis=0, keepdims=True),
                jnp.sum(my_times * block, axis=0, keepdims=True),
            ],
            axis=0,
        )

    blocks = []
    for p in range(n_panels):
        holder = jnp.full((s_dev, c_dev), owners_ref[p], jnp.int32)
        block = jnp.zeros((s_dev, c_dev), jnp.float32)
        for o in range(n_ch):
            block = jnp.where(holder == o, mine[:, o * c_dev : (o + 1) * c_dev], block)
        blocks.append(block)
    blocks = jnp.concatenate(blocks, axis=1)
    targets = jnp.concatenate(
        [local_ref[p : p + 1, :] + p * c_dev for p in range(n_panels)], axis=1
    )
    hot = (
        lax.broadcasted_iota(jnp.int32, (n_panels * c_dev, width), 0) == targets
    ).astype(jnp.float32)
    picked = jnp.dot(
        blocks, hot, precision=lax.Precision.HIGHEST, preferred_element_type=jnp.float32
    )
    rline[low, high] = jnp.concatenate([picked[:half], picked[half:]], axis=1)
    stat_in[me] = stat_out[me]

    pl.semaphore_wait(barrier, n_ch - 1 + n_seg - 1)

    s_copies = []
    for k in order:
        dst = (me + k) % n_ch
        s_copies.append(
            remote(stat_out.at[dst], stat_in.at[me], (s_send, s_recv), k, seg, dst)
        )
    z_copies = []
    for k in range(1, n_high):
        block = rline.at[low, high]
        dst = ((high + k) % n_high) * group + low
        z_copies.append(remote(block, block, (z_send, z_recv), k, seg, dst))
    a_copies = []
    for k in order:
        dst = (me + k) % n_ch
        block = strain_hbm.at[:, pl.ds(pl.multiple_of(dst * c_dev, LANES), c_dev)]
        a_copies.append(remote(block, raw.at[me], (a_send, a_recv), k, seg, dst))

    for copy in z_copies:
        copy.wait()
    p_copies = []
    for k in range(1, group):
        block = rline.at[low]
        dst = high * group + (low + k) % group
        p_copies.append(remote(block, block, (p_send, p_recv), k, seg, dst))

    for copy in s_copies:
        copy.wait()
    sums = jnp.sum(stat_in[...], axis=0)
    level_d = sums[0:1] / n_total
    slope_d = sums[1:2] / spread

    r_copies = []
    d_copies = []

    def forward(k):
        block = d_all.at[seg, (me - k + n_ch) % n_ch]
        for j in range(1, n_seg):
            d_copies.append(
                remote(block, block, (d_send.at[j], d_recv.at[j]), k, (seg + j) % n_seg, me)
            )

    ready = None
    for place, k in enumerate([0] + order):
        if k == 0:
            own.wait()
        else:
            a_copies[place - 1].wait()
        source = (me - k + n_ch) % n_ch
        times = (
            lax.broadcasted_iota(jnp.int32, (s_dev, c_dev), 0) + source * s_dev
        ).astype(jnp.float32) - mid_time
        d_all[seg, source] = (raw[source] - level_d - slope_d * times).astype(jnp.bfloat16)
        if ready is not None:
            forward(ready)
        ready = k
        if place == n_ch // 2:
            for copy in p_copies:
                copy.wait()
            rows = jnp.concatenate(
                [rline[i % group, i // group] for i in range(n_ch)], axis=0
            )
            row_id = lax.broadcasted_iota(jnp.int32, (n_ch * half, LANES), 0)
            upper = (
                lax.broadcasted_iota(jnp.int32, (n_ch * half, LANES), 1) >= width
            ).astype(jnp.int32)
            times = (row_id // half) * s_dev + row_id % half + upper * half
            centred = times.astype(jnp.float32) - mid_time
            level = jnp.sum(rows, axis=0, keepdims=True)
            slope = jnp.sum(centred * rows, axis=0, keepdims=True)
            level = (level + pltpu.roll(level, width, 1)) / n_total
            slope = (slope + pltpu.roll(slope, width, 1)) / spread
            r_all[seg] = (rows - level - slope * centred).astype(jnp.bfloat16)
        if place == n_ch // 2 + 1:
            block = r_all.at[seg]
            for j in range(1, n_seg):
                r_copies.append(
                    remote(block, block, (r_send, r_recv), j, (seg + j) % n_seg, me)
                )
    forward(ready)
    for copy in r_copies:
        copy.wait()
    r_out[...] = r_all[...]
    for copy in d_copies:
        copy.wait()
    d_out[...] = d_all[...].reshape(d_out.shape)


def lag_kernel(n_seg, half, d_ref, r_ref, out_ref, d_pad, shifted):
    lag_dev, width, c_dev = out_ref.shape
    n_total = d_ref.shape[1]
    n_ch = n_total // (2 * half)
    seg = lax.axis_index("seg")
    steps = lag_dev // SHIFTS
    d_pad[:, n_total:, :] = jnp.zeros((n_seg, L, c_dev), d_pad.dtype)
    d_pad[:, :n_total, :] = d_ref[...]
    shifted[:, : SHIFTS + 8, :] = jnp.zeros((n_seg, SHIFTS + 8, LANES), jnp.float32)
    lefts, rights = [], []
    for s in range(n_seg):
        packed = r_ref[s].astype(jnp.float32)
        swapped = pltpu.roll(packed, width, 1)
        both = jnp.concatenate(
            [packed.reshape(n_ch, half, LANES), swapped.reshape(n_ch, half, LANES)], axis=1
        ).reshape(n_total, LANES)
        turned = jnp.concatenate(
            [swapped.reshape(n_ch, half, LANES), packed.reshape(n_ch, half, LANES)], axis=1
        ).reshape(n_total, LANES)
        shifted[s, pl.ds(SHIFTS, n_total), 0:width] = both[:, :width]
        shifted[s, pl.ds(SHIFTS + 1, n_total), width:LANES] = turned[:, width:]
        lefts.append(
            jnp.concatenate(
                [
                    d_pad[
                        s,
                        pl.ds(pl.multiple_of(seg * lag_dev + a * SHIFTS, SHIFTS), n_total),
                        :,
                    ]
                    for a in range(steps)
                ],
                axis=1,
            )
        )
    base = (seg * lag_dev).astype(jnp.float32)
    quad = 4
    for j in range(SHIFTS // quad):
        total = None
        for s in range(n_seg):
            right = jnp.concatenate(
                [
                    shifted[s, pl.ds(SHIFTS - quad * j - b, n_total), :].astype(jnp.bfloat16)
                    for b in range(0, quad, 2)
                ],
                axis=1,
            )
            part = lax.dot_general(
                lefts[s], right, (((0,), (0,)), ((), ())), preferred_element_type=jnp.float32
            )
            total = part if total is None else total + part
        turned = total.T
        for a in range(steps):
            for b in range(quad):
                k = a * SHIFTS + j * quad + b
                block = turned[b * width : (b + 1) * width, a * c_dev : (a + 1) * c_dev]
                out_ref[k] = block / (n_seg * (n_total - (base + k)))


def wide_blocks(strain, ref_local, owners):
    my_rows = strain[0]
    s_dev, chans = my_rows.shape
    n_ch = lax.axis_size("ch")
    n_seg = lax.axis_size("seg")
    n_total = s_dev * n_ch
    c_dev = chans // n_ch
    half = s_dev // 2
    group = max(g for g in range(1, math.isqrt(n_ch) + 1) if n_ch % g == 0)
    n_high = n_ch // group
    width = ref_local.shape[0] * ref_local.shape[1]
    vmem = pl.BlockSpec(memory_space=pltpu.VMEM)
    dma = pltpu.SemaphoreType.DMA
    d_shape = (n_seg, n_total, c_dev)
    r_shape = (n_seg, n_ch * half, LANES)
    d_all, r_all = pl.pallas_call(
        functools.partial(exchange_kernel, n_seg, n_ch, group),
        out_shape=(
            jax.ShapeDtypeStruct(d_shape, jnp.bfloat16),
            jax.ShapeDtypeStruct(r_shape, jnp.bfloat16),
        ),
        in_specs=[
            pl.BlockSpec(memory_space=pl.ANY),
            pl.BlockSpec(memory_space=pltpu.SMEM),
            vmem,
        ],
        out_specs=(vmem, vmem),
        scratch_shapes=[
            pltpu.VMEM((s_dev, chans), jnp.float32),
            pltpu.VMEM((n_ch, s_dev, c_dev), jnp.float32),
            pltpu.VMEM((group, n_high, half, LANES), jnp.float32),
            pltpu.VMEM((n_seg, n_ch, s_dev, c_dev), jnp.bfloat16),
            pltpu.VMEM(r_shape, jnp.bfloat16),
            pltpu.VMEM((n_ch, 2, c_dev), jnp.float32),
            pltpu.VMEM((n_ch, 2, c_dev), jnp.float32),
            dma, dma,
            dma((n_ch,)), dma((n_ch,)),
            dma((n_ch,)), dma((n_ch,)),
            dma((n_high,)), dma((n_high,)),
            dma((group,)), dma((group,)),
            dma((n_seg, n_ch)), dma((n_seg, n_ch)),
            dma((n_seg,)), dma((n_seg,)),
        ],
        compiler_params=pltpu.CompilerParams(collective_id=0, has_side_effects=True, vmem_limit_bytes=GRANT),
    )(my_rows, owners, ref_local)
    turned = pl.pallas_call(
        functools.partial(lag_kernel, n_seg, half),
        out_shape=jax.ShapeDtypeStruct((L // n_seg, width, c_dev), jnp.float32),
        in_specs=[vmem, vmem],
        out_specs=vmem,
        scratch_shapes=[
            pltpu.VMEM((n_seg, n_total + L, c_dev), jnp.bfloat16),
            pltpu.VMEM((n_seg, SHIFTS + n_total + 8, LANES), jnp.float32),
        ],
        compiler_params=pltpu.CompilerParams(vmem_limit_bytes=GRANT),
    )(d_all, r_all)
    return turned.transpose(0, 2, 1)


def solution(mesh):
    n_seg, n_ch = mesh.shape["seg"], mesh.shape["ch"]

    def per_device(strain, ref_local, owners):
        s_dev, chans = strain.shape[1:]
        fits = (
            (chans // n_ch) % LANES == 0
            and (L // n_seg) % SHIFTS == 0
            and s_dev % 32 == 0
            and 2 * ref_local.size == LANES
        )
        return (wide_blocks if fits else narrow_blocks)(strain, ref_local, owners)

    in_specs = (P("seg", "ch", None), P(), P())
    out_specs = P("seg", "ch", None)
    return jax.shard_map(
        per_device, mesh=mesh, in_specs=in_specs, out_specs=out_specs, check_vma=False
    )
```

```python
import functools
import math

import jax
import jax.numpy as jnp
from jax import lax
from jax.experimental import pallas as pl
from jax.experimental.pallas import tpu as pltpu
from jax.sharding import PartitionSpec as P

L = 64
LANES = 128
SHIFTS = 16
GRANT = 24 * 1024 * 1024
MESH = pl.DeviceIdType.MESH


def spread_2(block, axis, holder):
    block = jnp.where(lax.axis_index(axis) == holder, block, jnp.zeros_like(block))
    return lax.psum(block, axis)


def detrend_cols(series):
    n_total = series.shape[0]
    mid_time = (n_total - 1) / 2.0
    spread = n_total * (n_total * n_total - 1) / 12.0
    centred = (jnp.arange(n_total, dtype=jnp.float32) - mid_time)[:, None]
    level_val = jnp.sum(series, axis=0) / n_total
    slope_val = jnp.sum(centred * series, axis=0) / spread
    return (series - level_val - slope_val * centred).astype(jnp.bfloat16)


def owner_panels(detrended, ref_local, owners):
    pieces = []
    for panel_id in range(ref_local.shape[0]):
        own_cols = jnp.take(detrended, ref_local[panel_id], axis=1)
        pieces.append(spread_2(own_cols, "ch", owners[panel_id]))
    return jnp.concatenate(pieces, axis=1)


def narrow_blocks(strain, ref_local, owners):
    my_rows = strain[0]
    s_dev, chans = my_rows.shape
    n_ch = lax.axis_size("ch")
    n_seg = lax.axis_size("seg")
    n_total = s_dev * n_ch
    c_dev = chans // n_ch
    series = lax.all_to_all(my_rows, "ch", split_axis=1, concat_axis=0, tiled=True)
    detrended = detrend_cols(series)
    panels = owner_panels(detrended, ref_local, owners)
    width_ref = panels.shape[1]
    padded = jnp.concatenate([detrended, jnp.zeros((L, c_dev), jnp.bfloat16)], axis=0)
    blk_rows = min(512, n_total)
    n_blocks = n_total // blk_rows
    lag_dev = L // n_seg
    lag_count = lax.axis_size("seg") * lag_dev

    def add_block(blk_idx, running):
        blk_start = blk_idx * blk_rows
        window = lax.dynamic_slice_in_dim(padded, blk_start, blk_rows + lag_count - 1, 0)
        lagged = jnp.concatenate(
            [window[lag_off : lag_off + blk_rows] for lag_off in range(lag_count)], axis=1
        )
        ref_block = lax.dynamic_slice_in_dim(panels, blk_start, blk_rows, 0)
        return running + lax.dot_general(
            lagged, ref_block, (((0,), (0,)), ((), ())), preferred_element_type=jnp.float32
        )

    start_acc = jnp.zeros((lag_count * c_dev, width_ref), jnp.float32)
    running = lax.fori_loop(0, n_blocks, add_block, start_acc)
    summed = lax.psum_scatter(
        running.reshape(lag_count, c_dev, width_ref), "seg", scatter_dimension=0, tiled=True
    )
    lag_ids = (lax.axis_index("seg") * lag_dev + jnp.arange(lag_dev, dtype=jnp.int32)).astype(
        jnp.float32
    )
    return summed / (n_seg * (n_total - lag_ids))[:, None, None]


def exchange_kernel(
    n_seg, n_ch, group,
    strain_hbm, owners_hbm, local_hbm, d_out, r_out,
    owners_ref, local_ref, mine, raw, rline, d_all, r_all, stat_out, stat_in,
    load_sem, own_sem, owners_sem, local_sem, s_send, s_recv, a_send, a_recv, z_send, z_recv, p_send, p_recv,
    d_send, d_recv, r_send, r_recv,
):
    seg = lax.axis_index("seg")
    me = lax.axis_index("ch")
    high, low = me // group, me % group
    n_high = n_ch // group
    s_dev = strain_hbm.shape[0]
    c_dev = strain_hbm.shape[1] // n_ch
    half = s_dev // 2
    n_total = s_dev * n_ch
    n_panels, panel_w = local_ref.shape
    width = n_panels * panel_w
    mid_time = (n_total - 1) / 2.0
    spread = n_total * (n_total * n_total - 1) / 12.0
    order = list(range(1, n_ch))

    def partner(k):
        place, bit = me, 1
        while bit <= k:
            if k & bit:
                place = place + (1 - 2 * ((me // bit) % 2)) * bit
            bit *= 2
        return place

    def remote(src, dst, sems, k, seg_to, ch_to):
        copy = pltpu.make_async_remote_copy(
            src_ref=src,
            dst_ref=dst,
            send_sem=sems[0].at[k],
            recv_sem=sems[1].at[k],
            device_id=(seg_to, ch_to),
            device_id_type=MESH,
        )
        copy.start()
        return copy

    barrier = pltpu.get_barrier_semaphore()
    for k in order:
        pl.semaphore_signal(
            barrier, inc=1, device_id=(seg, partner(k)), device_id_type=MESH
        )
    for k in range(1, n_seg):
        pl.semaphore_signal(
            barrier, inc=1, device_id=((seg + k) % n_seg, me), device_id_type=MESH
        )

    load = pltpu.make_async_copy(strain_hbm, mine, load_sem)
    load.start()
    load_owners = pltpu.make_async_copy(owners_hbm, owners_ref, owners_sem)
    load_owners.start()
    load_local = pltpu.make_async_copy(local_hbm, local_ref, local_sem)
    load_local.start()
    cols = pl.ds(pl.multiple_of(me * c_dev, LANES), c_dev)
    own = pltpu.make_async_copy(strain_hbm.at[:, cols], raw.at[me], own_sem)
    own.start()
    load.wait()

    my_times = (
        lax.broadcasted_iota(jnp.int32, (s_dev, c_dev), 0) + me * s_dev
    ).astype(jnp.float32) - mid_time
    for o in range(n_ch):
        block = mine[:, o * c_dev : (o + 1) * c_dev]
        stat_out[o] = jnp.concatenate(
            [
                jnp.sum(block, axis=0, keepdims=True),
                jnp.sum(my_times * block, axis=0, keepdims=True),
            ],
            axis=0,
        )

    load_owners.wait()
    load_local.wait()
    blocks = []
    for p in range(n_panels):
        holder = jnp.full((s_dev, c_dev), owners_ref[p], jnp.int32)
        block = jnp.zeros((s_dev, c_dev), jnp.float32)
        for o in range(n_ch):
            block = jnp.where(holder == o, mine[:, o * c_dev : (o + 1) * c_dev], block)
        blocks.append(block)
    blocks = jnp.concatenate(blocks, axis=1)
    targets = jnp.concatenate(
        [local_ref[p : p + 1, :] + p * c_dev for p in range(n_panels)], axis=1
    )
    hot = (
        lax.broadcasted_iota(jnp.int32, (n_panels * c_dev, width), 0) == targets
    ).astype(jnp.float32)
    picked = jnp.dot(
        blocks, hot, precision=lax.Precision.HIGHEST, preferred_element_type=jnp.float32
    )
    rline[low, high] = jnp.concatenate([picked[:half], picked[half:]], axis=1)
    stat_in[me] = stat_out[me]

    pl.semaphore_wait(barrier, n_ch - 1 + n_seg - 1)

    s_copies = []
    for k in order:
        dst = partner(k)
        s_copies.append(
            remote(stat_out.at[dst], stat_in.at[me], (s_send, s_recv), k, seg, dst)
        )
    z_copies = []
    for k in range(1, n_high):
        block = rline.at[low, high]
        dst = ((high + k) % n_high) * group + low
        z_copies.append(remote(block, block, (z_send, z_recv), k, seg, dst))
    a_copies = []
    for k in order:
        dst = partner(k)
        block = strain_hbm.at[:, pl.ds(pl.multiple_of(dst * c_dev, LANES), c_dev)]
        a_copies.append(remote(block, raw.at[me], (a_send, a_recv), k, seg, dst))

    for copy in z_copies:
        copy.wait()
    p_copies = []
    for k in range(1, group):
        block = rline.at[low]
        dst = high * group + (low + k) % group
        p_copies.append(remote(block, block, (p_send, p_recv), k, seg, dst))

    for copy in s_copies:
        copy.wait()
    sums = jnp.sum(stat_in[...], axis=0)
    level_d = sums[0:1] / n_total
    slope_d = sums[1:2] / spread

    r_copies = []
    d_copies = []

    def forward(k):
        block = d_all.at[seg, partner(k)]
        for j in range(1, n_seg):
            d_copies.append(
                remote(block, block, (d_send.at[j], d_recv.at[j]), k, (seg + j) % n_seg, me)
            )

    ready = None
    for place, k in enumerate([0] + order):
        if k == 0:
            own.wait()
        else:
            a_copies[place - 1].wait()
        source = partner(k)
        times = (
            lax.broadcasted_iota(jnp.int32, (s_dev, c_dev), 0) + source * s_dev
        ).astype(jnp.float32) - mid_time
        d_all[seg, source] = (raw[source] - level_d - slope_d * times).astype(jnp.bfloat16)
        if ready is not None:
            forward(ready)
        ready = k
        if place == n_ch // 2:
            for copy in p_copies:
                copy.wait()
            rows = jnp.concatenate(
                [rline[i % group, i // group] for i in range(n_ch)], axis=0
            )
            row_id = lax.broadcasted_iota(jnp.int32, (n_ch * half, LANES), 0)
            upper = (
                lax.broadcasted_iota(jnp.int32, (n_ch * half, LANES), 1) >= width
            ).astype(jnp.int32)
            times = (row_id // half) * s_dev + row_id % half + upper * half
            centred = times.astype(jnp.float32) - mid_time
            level = jnp.sum(rows, axis=0, keepdims=True)
            slope = jnp.sum(centred * rows, axis=0, keepdims=True)
            level = (level + pltpu.roll(level, width, 1)) / n_total
            slope = (slope + pltpu.roll(slope, width, 1)) / spread
            r_all[seg] = (rows - level - slope * centred).astype(jnp.bfloat16)
        if place == n_ch // 2 + 1:
            block = r_all.at[seg]
            for j in range(1, n_seg):
                r_copies.append(
                    remote(block, block, (r_send, r_recv), j, (seg + j) % n_seg, me)
                )
    forward(ready)
    for copy in r_copies:
        copy.wait()
    r_out[...] = r_all[...]
    for copy in d_copies:
        copy.wait()
    d_out[...] = d_all[...].reshape(d_out.shape)


def lag_kernel(n_seg, half, d_ref, r_ref, out_ref, d_pad, shifted):
    lag_dev, width, c_dev = out_ref.shape
    n_total = d_ref.shape[1]
    n_ch = n_total // (2 * half)
    seg = lax.axis_index("seg")
    steps = lag_dev // SHIFTS
    d_pad[:, n_total:, :] = jnp.zeros((n_seg, L, c_dev), d_pad.dtype)
    d_pad[:, :n_total, :] = d_ref[...]
    shifted[:, : SHIFTS + 8, :] = jnp.zeros((n_seg, SHIFTS + 8, LANES), jnp.float32)
    lefts, rights = [], []
    for s in range(n_seg):
        packed = r_ref[s].astype(jnp.float32)
        swapped = pltpu.roll(packed, width, 1)
        both = jnp.concatenate(
            [packed.reshape(n_ch, half, LANES), swapped.reshape(n_ch, half, LANES)], axis=1
        ).reshape(n_total, LANES)
        turned = jnp.concatenate(
            [swapped.reshape(n_ch, half, LANES), packed.reshape(n_ch, half, LANES)], axis=1
        ).reshape(n_total, LANES)
        shifted[s, pl.ds(SHIFTS, n_total), 0:width] = both[:, :width]
        shifted[s, pl.ds(SHIFTS + 1, n_total), width:LANES] = turned[:, width:]
        lefts.append(
            jnp.concatenate(
                [
                    d_pad[
                        s,
                        pl.ds(pl.multiple_of(seg * lag_dev + a * SHIFTS, SHIFTS), n_total),
                        :,
                    ]
                    for a in range(steps)
                ],
                axis=1,
            )
        )
    base = (seg * lag_dev).astype(jnp.float32)
    quad = 4
    for j in range(SHIFTS // quad):
        total = None
        for s in range(n_seg):
            right = jnp.concatenate(
                [
                    shifted[s, pl.ds(SHIFTS - quad * j - b, n_total), :].astype(jnp.bfloat16)
                    for b in range(0, quad, 2)
                ],
                axis=1,
            )
            part = lax.dot_general(
                lefts[s], right, (((0,), (0,)), ((), ())), preferred_element_type=jnp.float32
            )
            total = part if total is None else total + part
        turned = total.T
        for a in range(steps):
            for b in range(quad):
                k = a * SHIFTS + j * quad + b
                block = turned[b * width : (b + 1) * width, a * c_dev : (a + 1) * c_dev]
                out_ref[k] = block / (n_seg * (n_total - (base + k)))


def wide_blocks(strain, ref_local, owners):
    my_rows = strain[0]
    s_dev, chans = my_rows.shape
    n_ch = lax.axis_size("ch")
    n_seg = lax.axis_size("seg")
    n_total = s_dev * n_ch
    c_dev = chans // n_ch
    half = s_dev // 2
    group = max(g for g in range(1, math.isqrt(n_ch) + 1) if n_ch % g == 0)
    n_high = n_ch // group
    width = ref_local.shape[0] * ref_local.shape[1]
    vmem = pl.BlockSpec(memory_space=pltpu.VMEM)
    dma = pltpu.SemaphoreType.DMA
    d_shape = (n_seg, n_total, c_dev)
    r_shape = (n_seg, n_ch * half, LANES)
    d_all, r_all = pl.pallas_call(
        functools.partial(exchange_kernel, n_seg, n_ch, group),
        out_shape=(
            jax.ShapeDtypeStruct(d_shape, jnp.bfloat16),
            jax.ShapeDtypeStruct(r_shape, jnp.bfloat16),
        ),
        in_specs=[pl.BlockSpec(memory_space=pltpu.HBM)] * 3,
        out_specs=(vmem, vmem),
        scratch_shapes=[
            pltpu.SMEM(owners.shape, jnp.int32),
            pltpu.VMEM(ref_local.shape, jnp.int32),
            pltpu.VMEM((s_dev, chans), jnp.float32),
            pltpu.VMEM((n_ch, s_dev, c_dev), jnp.float32),
            pltpu.VMEM((group, n_high, half, LANES), jnp.float32),
            pltpu.VMEM((n_seg, n_ch, s_dev, c_dev), jnp.bfloat16),
            pltpu.VMEM(r_shape, jnp.bfloat16),
            pltpu.VMEM((n_ch, 2, c_dev), jnp.float32),
            pltpu.VMEM((n_ch, 2, c_dev), jnp.float32),
            dma, dma, dma, dma,
            dma((n_ch,)), dma((n_ch,)),
            dma((n_ch,)), dma((n_ch,)),
            dma((n_high,)), dma((n_high,)),
            dma((group,)), dma((group,)),
            dma((n_seg, n_ch)), dma((n_seg, n_ch)),
            dma((n_seg,)), dma((n_seg,)),
        ],
        compiler_params=pltpu.CompilerParams(collective_id=0, has_side_effects=True, vmem_limit_bytes=GRANT),
    )(my_rows, owners, ref_local)
    turned = pl.pallas_call(
        functools.partial(lag_kernel, n_seg, half),
        out_shape=jax.ShapeDtypeStruct((L // n_seg, width, c_dev), jnp.float32),
        in_specs=[vmem, vmem],
        out_specs=vmem,
        scratch_shapes=[
            pltpu.VMEM((n_seg, n_total + L, c_dev), jnp.bfloat16),
            pltpu.VMEM((n_seg, SHIFTS + n_total + 8, LANES), jnp.float32),
        ],
        compiler_params=pltpu.CompilerParams(vmem_limit_bytes=GRANT),
    )(d_all, r_all)
    return turned.transpose(0, 2, 1)


def solution(mesh):
    n_seg, n_ch = mesh.shape["seg"], mesh.shape["ch"]

    def per_device(strain, ref_local, owners):
        s_dev, chans = strain.shape[1:]
        fits = (
            (chans // n_ch) % LANES == 0
            and (L // n_seg) % SHIFTS == 0
            and s_dev % 32 == 0
            and n_ch & (n_ch - 1) == 0
            and 2 * ref_local.size == LANES
        )
        return (wide_blocks if fits else narrow_blocks)(strain, ref_local, owners)

    in_specs = (P("seg", "ch", None), P(), P())
    out_specs = P("seg", "ch", None)
    return jax.shard_map(
        per_device, mesh=mesh, in_specs=in_specs, out_specs=out_specs, check_vma=False
    )
```

```python
import functools
import math

import jax
import jax.numpy as jnp
from jax import lax
from jax.experimental import pallas as pl
from jax.experimental.pallas import tpu as pltpu
from jax.sharding import PartitionSpec as P

L = 64
LANES = 128
SHIFTS = 16
GRANT = 24 * 1024 * 1024
MESH = pl.DeviceIdType.MESH


def spread_2(block, axis, holder):
    block = jnp.where(lax.axis_index(axis) == holder, block, jnp.zeros_like(block))
    return lax.psum(block, axis)


def detrend_cols(series):
    n_total = series.shape[0]
    mid_time = (n_total - 1) / 2.0
    spread = n_total * (n_total * n_total - 1) / 12.0
    centred = (jnp.arange(n_total, dtype=jnp.float32) - mid_time)[:, None]
    level_val = jnp.sum(series, axis=0) / n_total
    slope_val = jnp.sum(centred * series, axis=0) / spread
    return (series - level_val - slope_val * centred).astype(jnp.bfloat16)


def owner_panels(detrended, ref_local, owners):
    pieces = []
    for panel_id in range(ref_local.shape[0]):
        own_cols = jnp.take(detrended, ref_local[panel_id], axis=1)
        pieces.append(spread_2(own_cols, "ch", owners[panel_id]))
    return jnp.concatenate(pieces, axis=1)


def narrow_blocks(strain, ref_local, owners):
    my_rows = strain[0]
    s_dev, chans = my_rows.shape
    n_ch = lax.axis_size("ch")
    n_seg = lax.axis_size("seg")
    n_total = s_dev * n_ch
    c_dev = chans // n_ch
    series = lax.all_to_all(my_rows, "ch", split_axis=1, concat_axis=0, tiled=True)
    detrended = detrend_cols(series)
    panels = owner_panels(detrended, ref_local, owners)
    width_ref = panels.shape[1]
    padded = jnp.concatenate([detrended, jnp.zeros((L, c_dev), jnp.bfloat16)], axis=0)
    blk_rows = min(512, n_total)
    n_blocks = n_total // blk_rows
    lag_dev = L // n_seg
    lag_count = lax.axis_size("seg") * lag_dev

    def add_block(blk_idx, running):
        blk_start = blk_idx * blk_rows
        window = lax.dynamic_slice_in_dim(padded, blk_start, blk_rows + lag_count - 1, 0)
        lagged = jnp.concatenate(
            [window[lag_off : lag_off + blk_rows] for lag_off in range(lag_count)], axis=1
        )
        ref_block = lax.dynamic_slice_in_dim(panels, blk_start, blk_rows, 0)
        return running + lax.dot_general(
            lagged, ref_block, (((0,), (0,)), ((), ())), preferred_element_type=jnp.float32
        )

    start_acc = jnp.zeros((lag_count * c_dev, width_ref), jnp.float32)
    running = lax.fori_loop(0, n_blocks, add_block, start_acc)
    summed = lax.psum_scatter(
        running.reshape(lag_count, c_dev, width_ref), "seg", scatter_dimension=0, tiled=True
    )
    lag_ids = (lax.axis_index("seg") * lag_dev + jnp.arange(lag_dev, dtype=jnp.int32)).astype(
        jnp.float32
    )
    return summed / (n_seg * (n_total - lag_ids))[:, None, None]


def exchange_kernel(
    n_seg, n_ch, group,
    strain_hbm, owners_hbm, local_hbm, d_out, r_out,
    owners_ref, local_ref, mine, raw, rline, d_all, r_all, stat_out, stat_in,
    load_sem, own_sem, owners_sem, local_sem, s_send, s_recv, a_send, a_recv, z_send, z_recv, p_send, p_recv,
    d_send, d_recv, r_send, r_recv, c_send, c_recv,
):
    seg = lax.axis_index("seg")
    me = lax.axis_index("ch")
    high, low = me // group, me % group
    n_high = n_ch // group
    s_dev = strain_hbm.shape[0]
    c_dev = strain_hbm.shape[1] // n_ch
    half = s_dev // 2
    n_total = s_dev * n_ch
    n_panels, panel_w = local_ref.shape
    width = n_panels * panel_w
    mid_time = (n_total - 1) / 2.0
    spread = n_total * (n_total * n_total - 1) / 12.0
    order = list(range(1, n_ch))

    def partner(k):
        place, bit = me, 1
        while bit <= k:
            if k & bit:
                place = place + (1 - 2 * ((me // bit) % 2)) * bit
            bit *= 2
        return place

    def remote(src, dst, sems, k, seg_to, ch_to):
        copy = pltpu.make_async_remote_copy(
            src_ref=src,
            dst_ref=dst,
            send_sem=sems[0].at[k],
            recv_sem=sems[1].at[k],
            device_id=(seg_to, ch_to),
            device_id_type=MESH,
        )
        copy.start()
        return copy

    barrier = pltpu.get_barrier_semaphore()
    for k in order:
        pl.semaphore_signal(
            barrier, inc=1, device_id=(seg, partner(k)), device_id_type=MESH
        )
    for k in range(1, n_seg):
        pl.semaphore_signal(
            barrier, inc=1, device_id=((seg + k) % n_seg, me), device_id_type=MESH
        )

    load = pltpu.make_async_copy(strain_hbm, mine, load_sem)
    load.start()
    load_owners = pltpu.make_async_copy(owners_hbm, owners_ref, owners_sem)
    load_owners.start()
    load_local = pltpu.make_async_copy(local_hbm, local_ref, local_sem)
    load_local.start()
    cols = pl.ds(pl.multiple_of(me * c_dev, LANES), c_dev)
    own = pltpu.make_async_copy(strain_hbm.at[:, cols], raw.at[me], own_sem)
    own.start()
    load.wait()

    my_times = (
        lax.broadcasted_iota(jnp.int32, (s_dev, c_dev), 0) + me * s_dev
    ).astype(jnp.float32) - mid_time
    for o in range(n_ch):
        block = mine[:, o * c_dev : (o + 1) * c_dev]
        stat_out[o] = jnp.concatenate(
            [
                jnp.sum(block, axis=0, keepdims=True),
                jnp.sum(my_times * block, axis=0, keepdims=True),
            ],
            axis=0,
        )

    load_owners.wait()
    load_local.wait()
    blocks = []
    for p in range(n_panels):
        holder = jnp.full((s_dev, c_dev), owners_ref[p], jnp.int32)
        block = jnp.zeros((s_dev, c_dev), jnp.float32)
        for o in range(n_ch):
            block = jnp.where(holder == o, mine[:, o * c_dev : (o + 1) * c_dev], block)
        blocks.append(block)
    blocks = jnp.concatenate(blocks, axis=1)
    targets = jnp.concatenate(
        [local_ref[p : p + 1, :] + p * c_dev for p in range(n_panels)], axis=1
    )
    hot = (
        lax.broadcasted_iota(jnp.int32, (n_panels * c_dev, width), 0) == targets
    ).astype(jnp.float32)
    picked = jnp.dot(
        blocks, hot, precision=lax.Precision.HIGHEST, preferred_element_type=jnp.float32
    )
    rline[low, high] = jnp.concatenate([picked[:half], picked[half:]], axis=1)
    stat_in[me] = stat_out[me]

    pl.semaphore_wait(barrier, n_ch - 1 + n_seg - 1)

    s_copies = []
    for k in order:
        dst = partner(k)
        s_copies.append(
            remote(stat_out.at[dst], stat_in.at[me], (s_send, s_recv), k, seg, dst)
        )
    z_copies = []
    for k in range(1, n_high):
        block = rline.at[low, high]
        dst = ((high + k) % n_high) * group + low
        z_copies.append(remote(block, block, (z_send, z_recv), k, seg, dst))
    a_copies = []
    for k in order:
        dst = partner(k)
        block = strain_hbm.at[:, pl.ds(pl.multiple_of(dst * c_dev, LANES), c_dev)]
        a_copies.append(remote(block, raw.at[me], (a_send, a_recv), k, seg, dst))

    for copy in z_copies:
        copy.wait()
    p_copies = []
    for k in range(1, group):
        block = rline.at[low]
        dst = high * group + (low + k) % group
        p_copies.append(remote(block, block, (p_send, p_recv), k, seg, dst))

    for copy in s_copies:
        copy.wait()
    sums = jnp.sum(stat_in[...], axis=0)
    level_d = sums[0:1] / n_total
    slope_d = sums[1:2] / spread

    r_copies = []
    d_copies = []

    def forward(k):
        block = d_all.at[seg, partner(k)]
        for j in range(1, n_seg):
            d_copies.append(
                remote(block, block, (d_send.at[j], d_recv.at[j]), k, (seg + j) % n_seg, me)
            )

    ready = None
    for place, k in enumerate([0] + order):
        if k == 0:
            own.wait()
        else:
            a_copies[place - 1].wait()
        source = partner(k)
        times = (
            lax.broadcasted_iota(jnp.int32, (s_dev, c_dev), 0) + source * s_dev
        ).astype(jnp.float32) - mid_time
        d_all[seg, source] = (raw[source] - level_d - slope_d * times).astype(jnp.bfloat16)
        if ready is not None:
            forward(ready)
        ready = k
        if place == n_ch // 2:
            for copy in p_copies:
                copy.wait()
            rows = jnp.concatenate(
                [rline[i % group, i // group] for i in range(n_ch)], axis=0
            )
            row_id = lax.broadcasted_iota(jnp.int32, (n_ch * half, LANES), 0)
            upper = (
                lax.broadcasted_iota(jnp.int32, (n_ch * half, LANES), 1) >= width
            ).astype(jnp.int32)
            times = (row_id // half) * s_dev + row_id % half + upper * half
            centred = times.astype(jnp.float32) - mid_time
            level = jnp.sum(rows, axis=0, keepdims=True)
            slope = jnp.sum(centred * rows, axis=0, keepdims=True)
            level = (level + pltpu.roll(level, width, 1)) / n_total
            slope = (slope + pltpu.roll(slope, width, 1)) / spread
            r_all[seg] = (
                (rows - level - slope * centred).astype(jnp.bfloat16).reshape(r_all.shape[1:])
            )
        if place == n_ch // 2 + 1:
            block = r_all.at[seg, me % 2]
            for j in range(1, n_seg):
                r_copies.append(
                    remote(block, block, (r_send, r_recv), j, (seg + j) % n_seg, me)
                )
    forward(ready)
    c_copies = []
    for j, copy in enumerate(r_copies, 1):
        copy.wait()
        block = r_all.at[(seg - j + n_seg) % n_seg, me % 2]
        c_copies.append(remote(block, block, (c_send, c_recv), j, seg, partner(1)))
    for copy in c_copies:
        copy.wait()
    r_out[...] = r_all[...].reshape(r_out.shape)
    for copy in d_copies:
        copy.wait()
    d_out[...] = d_all[...].reshape(d_out.shape)


def lag_kernel(n_seg, half, d_ref, r_ref, out_ref, d_pad, shifted):
    lag_dev, width, c_dev = out_ref.shape
    n_total = d_ref.shape[1]
    n_ch = n_total // (2 * half)
    seg = lax.axis_index("seg")
    steps = lag_dev // SHIFTS
    d_pad[:, n_total:, :] = jnp.zeros((n_seg, L, c_dev), d_pad.dtype)
    d_pad[:, :n_total, :] = d_ref[...]
    shifted[:, : SHIFTS + 8, :] = jnp.zeros((n_seg, SHIFTS + 8, LANES), jnp.float32)
    lefts, rights = [], []
    for s in range(n_seg):
        packed = r_ref[s].astype(jnp.float32)
        swapped = pltpu.roll(packed, width, 1)
        both = jnp.concatenate(
            [packed.reshape(n_ch, half, LANES), swapped.reshape(n_ch, half, LANES)], axis=1
        ).reshape(n_total, LANES)
        turned = jnp.concatenate(
            [swapped.reshape(n_ch, half, LANES), packed.reshape(n_ch, half, LANES)], axis=1
        ).reshape(n_total, LANES)
        shifted[s, pl.ds(SHIFTS, n_total), 0:width] = both[:, :width]
        shifted[s, pl.ds(SHIFTS + 1, n_total), width:LANES] = turned[:, width:]
        lefts.append(
            jnp.concatenate(
                [
                    d_pad[
                        s,
                        pl.ds(pl.multiple_of(seg * lag_dev + a * SHIFTS, SHIFTS), n_total),
                        :,
                    ]
                    for a in range(steps)
                ],
                axis=1,
            )
        )
    base = (seg * lag_dev).astype(jnp.float32)
    quad = 4
    for j in range(SHIFTS // quad):
        total = None
        for s in range(n_seg):
            right = jnp.concatenate(
                [
                    shifted[s, pl.ds(SHIFTS - quad * j - b, n_total), :].astype(jnp.bfloat16)
                    for b in range(0, quad, 2)
                ],
                axis=1,
            )
            part = lax.dot_general(
                lefts[s], right, (((0,), (0,)), ((), ())), preferred_element_type=jnp.float32
            )
            total = part if total is None else total + part
        turned = total.T
        for a in range(steps):
            for b in range(quad):
                k = a * SHIFTS + j * quad + b
                block = turned[b * width : (b + 1) * width, a * c_dev : (a + 1) * c_dev]
                out_ref[k] = block / (n_seg * (n_total - (base + k)))


def wide_blocks(strain, ref_local, owners):
    my_rows = strain[0]
    s_dev, chans = my_rows.shape
    n_ch = lax.axis_size("ch")
    n_seg = lax.axis_size("seg")
    n_total = s_dev * n_ch
    c_dev = chans // n_ch
    half = s_dev // 2
    group = max(g for g in range(1, math.isqrt(n_ch) + 1) if n_ch % g == 0)
    n_high = n_ch // group
    width = ref_local.shape[0] * ref_local.shape[1]
    vmem = pl.BlockSpec(memory_space=pltpu.VMEM)
    dma = pltpu.SemaphoreType.DMA
    d_shape = (n_seg, n_total, c_dev)
    r_shape = (n_seg, n_ch * half, LANES)
    d_all, r_all = pl.pallas_call(
        functools.partial(exchange_kernel, n_seg, n_ch, group),
        out_shape=(
            jax.ShapeDtypeStruct(d_shape, jnp.bfloat16),
            jax.ShapeDtypeStruct(r_shape, jnp.bfloat16),
        ),
        in_specs=[pl.BlockSpec(memory_space=pltpu.HBM)] * 3,
        out_specs=(vmem, vmem),
        scratch_shapes=[
            pltpu.SMEM(owners.shape, jnp.int32),
            pltpu.VMEM(ref_local.shape, jnp.int32),
            pltpu.VMEM((s_dev, chans), jnp.float32),
            pltpu.VMEM((n_ch, s_dev, c_dev), jnp.float32),
            pltpu.VMEM((group, n_high, half, LANES), jnp.float32),
            pltpu.VMEM((n_seg, n_ch, s_dev, c_dev), jnp.bfloat16),
            pltpu.VMEM((n_seg, 2, n_ch * half // 2, LANES), jnp.bfloat16),
            pltpu.VMEM((n_ch, 2, c_dev), jnp.float32),
            pltpu.VMEM((n_ch, 2, c_dev), jnp.float32),
            dma, dma, dma, dma,
            dma((n_ch,)), dma((n_ch,)),
            dma((n_ch,)), dma((n_ch,)),
            dma((n_high,)), dma((n_high,)),
            dma((group,)), dma((group,)),
            dma((n_seg, n_ch)), dma((n_seg, n_ch)),
            dma((n_seg,)), dma((n_seg,)),
            dma((n_seg,)), dma((n_seg,)),
        ],
        compiler_params=pltpu.CompilerParams(collective_id=0, has_side_effects=True, vmem_limit_bytes=GRANT),
    )(my_rows, owners, ref_local)
    turned = pl.pallas_call(
        functools.partial(lag_kernel, n_seg, half),
        out_shape=jax.ShapeDtypeStruct((L // n_seg, width, c_dev), jnp.float32),
        in_specs=[vmem, vmem],
        out_specs=vmem,
        scratch_shapes=[
            pltpu.VMEM((n_seg, n_total + L, c_dev), jnp.bfloat16),
            pltpu.VMEM((n_seg, SHIFTS + n_total + 8, LANES), jnp.float32),
        ],
        compiler_params=pltpu.CompilerParams(vmem_limit_bytes=GRANT),
    )(d_all, r_all)
    return turned.transpose(0, 2, 1)


def solution(mesh):
    n_seg, n_ch = mesh.shape["seg"], mesh.shape["ch"]

    def per_device(strain, ref_local, owners):
        s_dev, chans = strain.shape[1:]
        fits = (
            (chans // n_ch) % LANES == 0
            and (L // n_seg) % SHIFTS == 0
            and s_dev % 32 == 0
            and n_ch % 2 == 0
            and n_ch & (n_ch - 1) == 0
            and 2 * ref_local.size == LANES
        )
        return (wide_blocks if fits else narrow_blocks)(strain, ref_local, owners)

    in_specs = (P("seg", "ch", None), P(), P())
    out_specs = P("seg", "ch", None)
    return jax.shard_map(
        per_device, mesh=mesh, in_specs=in_specs, out_specs=out_specs, check_vma=False
    )
```
